32 devices in a mesh: ctx: 16 (over z, x, core), head: 2 (over y).
Axes of the slice: x: 2, y: 2, z: 4, core: 2. Of those that a mesh axis runs over, the one named last changes fastest.
Arguments:
- query_rows: bfloat16 [8192, 2048], P('ctx', 'head'), may hold values from -60 to 60
- key_rows: bfloat16 [8192, 2048], P('ctx', 'head'), may hold values from -6 to 6
- value_rows: bfloat16 [8192, 2048], P('ctx', 'head'), may hold values from -60 to 60
- log_gate: float32 [16, 8192], P('head', 'ctx'), may hold values from -0.5 to 0
- conv_weight: float32 [3, 4, 2048], P(None, None, 'head'), may hold values from -3 to 3
- norm_gain: float32 [2048], P('head'), may hold values from 0.5 to 1.5
- mixed_grad: bfloat16 [8192, 2048], P('ctx', 'head'), may hold values from -24 to 24
Outputs:
- mixer_out: bfloat16 [8192, 2048], P('ctx', 'head')
- query_grad: bfloat16 [8192, 2048], P('ctx', 'head')
- key_grad: bfloat16 [8192, 2048], P('ctx', 'head')
- value_grad: bfloat16 [8192, 2048], P('ctx', 'head')
- conv_grad: float32 [3, 4, 2048], P(None, None, 'head')
- gain_grad: float32 [2048], P('head')
The draws below stay inside these ranges and needn't reach their ends.
All inputs are finite; a program needn't handle non-finite values.
Results may differ from the reference program's by a relative error of at most 0.015.
Values may be sent and summed in bfloat16 or wider, within the bound.
A program may use at most 128 MiB of HBM per device.

```python
import math
import jax
import jax.numpy as jnp
from jax import lax

HD = 128
HEADS = 16
TAPS = 4
GROUP = 512
D = 2048
TOKENS = 8192


def draw_query_rows(key, part):
    inner_key = jax.random.fold_in(key, 11)
    noise_key, scale_key = jax.random.split(inner_key)
    noise_part = jnp.clip(jax.random.normal(noise_key, (TOKENS, D), jnp.float32), -6.0, 6.0)
    scales = jnp.exp(jax.random.uniform(scale_key, (TOKENS, HEADS), jnp.float32, 0.0, math.log(10.0)))
    return (noise_part * jnp.repeat(scales, HD, axis=1)).astype(jnp.bfloat16)


def draw_value_rows(key, part):
    inner_key = jax.random.fold_in(key, 12)
    ramp = jnp.arange(HEADS).astype(jnp.float32) / (HEADS - 1)
    noise_part = jnp.clip(jax.random.normal(inner_key, (TOKENS, D), jnp.float32), -6.0, 6.0)
    scales = jnp.power(10.0, ramp)
    return (noise_part * jnp.repeat(scales, HD)[None, :]).astype(jnp.bfloat16)


def draw_mixed_grad(key, part):
    inner_key = jax.random.fold_in(key, 13)
    noise_key = jax.random.fold_in(inner_key, 0)
    ramp = jnp.arange(TOKENS).astype(jnp.float32) / (TOKENS - 1)
    noise_part = jnp.clip(jax.random.normal(noise_key, (TOKENS, D), jnp.float32), -6.0, 6.0)
    result = noise_part * jnp.power(3.0, ramp)[:, None]
    return result.astype(jnp.bfloat16)


def draw_log_gate(key, part):
    inner_key = jax.random.fold_in(key, 14)
    keys_all = jax.random.split(inner_key, 6)
    picker = jax.random.uniform(keys_all[0], (HEADS,), jnp.float32)
    is_fast = picker < 0.5
    slow_rate = jnp.exp(jax.random.uniform(keys_all[2], (HEADS,), jnp.float32, math.log(0.1), math.log(0.8))) / TOKENS
    fast_rate = jnp.exp(jax.random.uniform(keys_all[1], (HEADS,), jnp.float32, math.log(1.0 / 50.0), math.log(1.0 / 30.0)))
    head_rate = jnp.where(is_fast, fast_rate, slow_rate)
    jitter = jnp.exp(jax.random.uniform(keys_all[3], (HEADS, TOKENS), jnp.float32, math.log(0.5), math.log(2.0)))
    positions = jax.random.randint(keys_all[4], (3,), 0, TOKENS)
    hit_mask = jnp.any(jnp.arange(TOKENS)[None, :] == positions[:, None], axis=0)
    losses = jax.random.uniform(keys_all[5], (HEADS, TOKENS), jnp.float32, 0.2, 0.3)
    return -head_rate[:, None] * jitter + jnp.where(hit_mask[None, :], jnp.log(1.0 - losses), 0.0)


def steps_of(stream_key, dims, shards, low, top_value):
    def one(position, parts):
        heights = jax.random.uniform(jax.random.fold_in(jax.random.fold_in(stream_key, 6), position), (parts,), jnp.float32, low / len(shards), top_value / len(shards))
        return jnp.repeat(jnp.exp(heights), dims[position] // parts).reshape((-1,) + (1,) * (len(dims) - position - 1))

    gain = one(*shards[0])
    for cut in shards[1:]:
        gain = gain * one(*cut)
    return gain


def gaussian(own_key, dims, width, limit, pieces=(), kind=jnp.bfloat16):
    values = jax.random.normal(own_key, dims, jnp.float32) * width
    if len(pieces) > 0:
        values = steps_of(own_key, dims, pieces, -0.22, 0.18) * values
    return jnp.clip(values, min=-limit, max=limit).astype(kind)


def setup_inputs(seed: int = 0) -> dict:
    key_of = jax.random.split(jax.random.key(seed), 8)
    return {
        "query_rows": draw_query_rows(jax.random.fold_in(key_of[7], 71), 0),
        "key_rows": gaussian(key_of[1], (TOKENS, D), 1.0, 6.0, ((0, 16), (1, 2))),
        "value_rows": draw_value_rows(jax.random.fold_in(key_of[7], 71), 0),
        "log_gate": draw_log_gate(jax.random.fold_in(key_of[7], 71), 0),
        "conv_weight": gaussian(key_of[4], (3, TAPS, D), 0.5, 3.0, ((2, 2),), jnp.float32),
        "norm_gain": jnp.clip(1.0 + 0.1 * jax.random.normal(key_of[5], (D,), jnp.float32), 0.5, 1.5),
        "mixed_grad": draw_mixed_grad(jax.random.fold_in(key_of[7], 71), 0),
    }


norm_epsilon = 1e-05
highest = lax.Precision.HIGHEST

def lowered(values):
    return lax.optimization_barrier(values.astype(jnp.bfloat16)).astype(jnp.float32)

def conv_forward(rows, weight):
    wide = rows.astype(jnp.float32)
    result = weight[0][None, :] * wide
    for offset in range(1, TAPS):
        moved = jnp.concatenate([jnp.zeros((offset, wide.shape[1]), jnp.float32), wide[:-offset]], axis=0)
        result = result + weight[offset][None, :] * moved
    return result.astype(jnp.bfloat16)

def conv_backward(grad_rows, rows, weight):
    wide = rows.astype(jnp.float32)
    input_grad = weight[0][None, :] * grad_rows
    weight_grad = [lax.optimization_barrier(jnp.sum(grad_rows * wide, axis=0))]
    for offset in range(1, TAPS):
        ahead = jnp.concatenate([grad_rows[offset:], jnp.zeros((offset, wide.shape[1]), jnp.float32)], axis=0)
        input_grad = input_grad + weight[offset][None, :] * ahead
        behind = jnp.concatenate([jnp.zeros((offset, wide.shape[1]), jnp.float32), wide[:-offset]], axis=0)
        weight_grad.append(lax.optimization_barrier(jnp.sum(grad_rows * behind, axis=0)))
    return (input_grad.astype(jnp.bfloat16), jnp.stack(weight_grad))

def decay_tables(gate_blocks):
    running = jnp.cumsum(gate_blocks, axis=-1)
    closing = running[..., -1]
    gap_matrix = running[..., :, None] - running[..., None, :]
    block_size = gate_blocks.shape[-1]
    lower_mask = jnp.arange(block_size)[:, None] >= jnp.arange(block_size)[None, :]
    weights = jnp.where(lower_mask, jnp.exp(jnp.minimum(gap_matrix, 0.0)), 0.0)
    return (running, closing, weights)

def reference(query_rows, key_rows, value_rows, log_gate, conv_weight, norm_gain, mixed_grad):
    query_conv = conv_forward(query_rows, conv_weight[0])
    key_conv = conv_forward(key_rows, conv_weight[1])
    value_conv = conv_forward(value_rows, conv_weight[2])
    block_count = TOKENS // GROUP

    def blocked(rows):
        return rows.astype(jnp.float32).reshape(block_count, GROUP, HEADS, HD)
    query_blocks = blocked(query_conv)
    key_blocks = blocked(key_conv)
    value_blocks = blocked(value_conv)
    gate_blocks = log_gate.reshape(HEADS, block_count, GROUP).transpose(1, 0, 2)

    def forward_step(state, inputs):
        query_here, key_here, value_here, gate_here = inputs
        running, closing, weights = decay_tables(gate_here)
        grow_factor = jnp.exp(running).T[:, :, None]
        shrink = jnp.exp(closing[:, None] - running).T[:, :, None]
        scores = jnp.einsum('thd,shd->hts', query_here, key_here, precision=highest)
        weights_low = lowered(scores * weights)
        state_low = lowered(state)
        attended = jnp.einsum('hts,she->the', weights_low, value_here, precision=highest)
        attended = attended + jnp.einsum('thd,hde->the', query_here, state_low, precision=highest) * grow_factor
        key_scaled = lowered(key_here * shrink)
        new_state = jnp.exp(closing)[:, None, None] * state + jnp.einsum('shd,she->hde', key_scaled, value_here, precision=highest)
        return (new_state, (attended, state))
    zero_state = jnp.zeros((HEADS, HD, HD), jnp.float32)
    last_state, (attended, states_in) = lax.scan(forward_step, zero_state, (query_blocks, key_blocks, value_blocks, gate_blocks))
    attended = attended.reshape(TOKENS, D)
    inverse = lax.rsqrt(lax.optimization_barrier(jnp.mean(attended * attended, axis=1)) + norm_epsilon)
    normed = attended * inverse[:, None]
    mixer_out = (normed * norm_gain[None, :]).astype(jnp.bfloat16)
    grad_wide = mixed_grad.astype(jnp.float32)
    gain_grad = lax.optimization_barrier(jnp.sum(grad_wide * normed, axis=0))
    scaled = grad_wide * norm_gain[None, :]
    inner_sum = lax.optimization_barrier(jnp.mean(scaled * attended, axis=1))
    out_grad = (inverse[:, None] * (scaled - attended * (inverse * inverse * inner_sum)[:, None])).astype(jnp.bfloat16)
    grad_blocks = blocked(out_grad)

    def backward_step(later_state, inputs):
        query_here, key_here, value_here, grad_here, gate_here, state_here = inputs
        running, closing, weights = decay_tables(gate_here)
        grow_factor = jnp.exp(running).T[:, :, None]
        shrink = jnp.exp(closing[:, None] - running).T[:, :, None]
        scores = jnp.einsum('thd,shd->hts', query_here, key_here, precision=highest)
        weights_low = lowered(scores * weights)
        state_low = lowered(state_here)
        later_low = lowered(later_state)
        grad_scores = lowered(jnp.einsum('the,she->hts', grad_here, value_here, precision=highest) * weights)
        query_part = jnp.einsum('hts,shd->thd', grad_scores, key_here, precision=highest)
        query_part = query_part + jnp.einsum('the,hde->thd', grad_here, state_low, precision=highest) * grow_factor
        key_part = jnp.einsum('hts,thd->shd', grad_scores, query_here, precision=highest)
        key_part = key_part + jnp.einsum('she,hde->shd', value_here, later_low, precision=highest) * shrink
        value_part = jnp.einsum('hts,the->she', weights_low, grad_here, precision=highest)
        value_part = value_part + jnp.einsum('shd,hde->she', key_here, later_low, precision=highest) * shrink
        query_scaled = lowered(query_here * grow_factor)
        new_later = jnp.exp(closing)[:, None, None] * later_state + jnp.einsum('thd,the->hde', query_scaled, grad_here, precision=highest)
        return (new_later, (query_part, key_part, value_part))
    first_later, (query_cg, key_cg, value_cg) = lax.scan(backward_step, zero_state, (query_blocks, key_blocks, value_blocks, grad_blocks, gate_blocks, states_in), reverse=True)
    query_grad, query_taps = conv_backward(query_cg.reshape(TOKENS, D), query_rows, conv_weight[0])
    key_grad, key_taps = conv_backward(key_cg.reshape(TOKENS, D), key_rows, conv_weight[1])
    value_grad, value_taps = conv_backward(value_cg.reshape(TOKENS, D), value_rows, conv_weight[2])
    conv_grad = jnp.stack([query_taps, key_taps, value_taps])
    return (mixer_out, query_grad, key_grad, value_grad, conv_grad, gain_grad)
```

```python
import functools

import jax
import jax.numpy as jnp
from jax import lax
from jax.experimental import pallas as pl
from jax.experimental.pallas import tpu as pltpu
from jax.sharding import PartitionSpec as P

HD = 128
TAPS = 4
GROUP = 512
HALF = GROUP // 2
PAD = 16
EPS = 1e-05
MESH = pl.DeviceIdType.MESH
F32 = jnp.float32
BF16 = jnp.bfloat16


def dot_nn(a, b):
    return lax.dot_general(a, b, (((1,), (0,)), ((), ())), preferred_element_type=F32)


def dot_nt(a, b):
    return lax.dot_general(a, b, (((1,), (1,)), ((), ())), preferred_element_type=F32)


def dot_tn(a, b):
    return lax.dot_general(a, b, (((0,), (0,)), ((), ())), preferred_element_type=F32)


def kernel(
    n, m, heads, owners,
    q_hbm, k_hbm, v_hbm, g_hbm, lg_ref, w_ref, gain_ref,
    mix_hbm, qg_hbm, kg_hbm, vg_hbm, cgrad_ref, ggrad_ref,
    ext, xf, qc, kc, vc, gb, att, og, mixb, outb, cg,
    w0, w1, p0, p1, colb, rowb, closb, closr,
    fs, fr, fo, fi, bs, br, bo, bi,
    accs, acci, invb, coefb, hs_tx, hs_rx,
    tap, tapr, tsum, tapo,
    loc, ha_s, ha_r, cl_s, cl_r,
    f1_s, f1_r, f2_s, f2_r, b1_s, b1_r, b2_s, b2_r,
    hs_s, hs_r, eh_s, eh_r, t1_s, t1_r, t2_s, t2_r,
):
    me = lax.axis_index("ctx")
    hme = lax.axis_index("head")
    per = owners // heads
    R = HD // per
    tiles = 2 * heads
    width = heads * HD
    total = width * m
    convs = (qc, kc, vc)

    def ctx_copy(src, dst, ss, rs, p):
        return pltpu.make_async_remote_copy(
            src_ref=src, dst_ref=dst, send_sem=ss, recv_sem=rs,
            device_id={"ctx": p}, device_id_type=MESH,
        )

    def head_copy(src, dst, ss, rs, p):
        return pltpu.make_async_remote_copy(
            src_ref=src, dst_ref=dst, send_sem=ss, recv_sem=rs,
            device_id={"head": p}, device_id_type=MESH,
        )

    def peers(count, fn):
        def one(d, c):
            p = lax.rem(me + d, n)
            if count == n:
                fn(p)
            else:
                pl.when(p < count)(lambda: fn(p))
            return c

        lax.fori_loop(1, n, one, 0)

    def owning(count, fn):
        if count == n:
            fn()
        else:
            pl.when(me < count)(fn)

    def cols_of(h):
        return pl.ds(pl.multiple_of(h * HD, HD), HD)

    ins = [
        pltpu.make_async_copy(src, ext.at[c, pl.ds(PAD, GROUP), :], loc.at[c])
        for c, src in enumerate((q_hbm, k_hbm, v_hbm))
    ]
    ins.append(pltpu.make_async_copy(g_hbm, gb, loc.at[3]))
    for cp in ins:
        cp.start()

    barrier = pltpu.get_barrier_semaphore()

    def greet(p):
        pl.semaphore_signal(barrier, inc=1, device_id={"ctx": p}, device_id_type=MESH)

    peers(n, greet)
    for d in range(1, m):
        pl.semaphore_signal(
            barrier, inc=1, device_id={"head": lax.rem(hme + d, m)}, device_id_type=MESH
        )

    run = lg_ref[...]
    lane = lax.broadcasted_iota(jnp.int32, run.shape, 1)
    d = 1
    while d < GROUP:
        run = run + jnp.where(lane >= d, pltpu.roll(run, d, 1), 0.0)
        d *= 2
    run_t = run.T
    for h in range(heads):
        colb[h] = jnp.broadcast_to(run_t[:, h : h + 1], (GROUP, HD))
        rowb[h] = jnp.broadcast_to(run[h : h + 1, :], (8, GROUP))
        closb[h] = jnp.broadcast_to(run[h : h + 1, GROUP - 1 : GROUP], (8, HD))

    tap[...] = jnp.zeros_like(tap)
    hs_tx[...] = jnp.zeros_like(hs_tx)

    pl.semaphore_wait(barrier, n - 1 + m - 1)

    rows_in = (q_hbm, k_hbm, v_hbm)

    def halo(c):
        return ctx_copy(
            rows_in[c].at[pl.ds(GROUP - PAD, PAD), :], ext.at[c, pl.ds(0, PAD), :],
            ha_s.at[c], ha_r.at[c], lax.rem(me + 1, n),
        )

    @pl.when(me < n - 1)
    def _():
        for c in (1, 2, 0):
            halo(c).start()

    @pl.when(me == 0)
    def _():
        ext[:, pl.ds(0, PAD), :] = jnp.zeros((3, PAD, width), BF16)

    def clos_copy(p, source):
        return ctx_copy(closb.at[p // per], closr.at[source], cl_s.at[p], cl_r.at[source], p)

    peers(owners, lambda p: clos_copy(p, me).start())

    def own_clos():
        closr[me] = closb[me // per]

    owning(owners, own_clos)

    def decay(h, c):
        col = colb[h]
        row = rowb[h][0:1, :]
        top = jnp.concatenate([col[:HALF]] * 2, axis=1)
        low = jnp.concatenate([col[HALF:]] * 2, axis=1)
        keep = lax.broadcasted_iota(jnp.int32, (HALF, HALF), 0) >= lax.broadcasted_iota(
            jnp.int32, (HALF, HALF), 1
        )
        w0[h] = jnp.where(keep, jnp.exp(jnp.minimum(top - row[:, :HALF], 0.0)), 0.0)
        w1[h, :, :HALF] = jnp.exp(jnp.minimum(low - row[:, :HALF], 0.0))
        w1[h, :, HALF:] = jnp.where(keep, jnp.exp(jnp.minimum(low - row[:, HALF:], 0.0)), 0.0)
        return c

    lax.fori_loop(0, heads, decay, 0)

    for cp in ins:
        cp.wait()

    @pl.when(me > 0)
    def _():
        for c in range(3):
            halo(c).wait_recv()

    def conv(c, h):
        cols = cols_of(h)
        xf[c, :, cols] = ext[c, :, cols].astype(F32)
        y = w_ref[c, 0:1, cols] * xf[c, pl.ds(PAD, GROUP), cols]
        for j in range(1, TAPS):
            y = y + w_ref[c, j : j + 1, cols] * xf[c, pl.ds(PAD - j, GROUP), cols]
        convs[c][:, cols] = y.astype(BF16)

    def shrink_of(h):
        return jnp.exp(closb[h][0:1, :] - colb[h])

    def slice_copy(src, dst, ss, rs, o, source):
        return ctx_copy(src.at[o], dst.at[source], ss.at[o], rs.at[source], o)

    def hand_out(state, h, src, dst, ss, rs):
        state = state.astype(BF16)
        for i in range(per):
            o = h * per + i
            src[o] = state[i * R : (i + 1) * R]

            @pl.when(o != me)
            def _():
                slice_copy(src, dst, ss, rs, o, me).start()

            @pl.when(o == me)
            def _():
                dst[me] = state[i * R : (i + 1) * R]

    def scan_slices(backwards, src, ss, got, rs, out, res, ss2, rs2):
        def take():
            peers(n, lambda s: slice_copy(src, got, ss, rs, 0, s).wait_recv())

            def step(i, state):
                b = n - 1 - i if backwards else i
                out[b] = state.astype(BF16)
                return jnp.exp(closr[b][0:1, :]) * state + got[b].astype(F32)

            lax.fori_loop(0, n, step, jnp.zeros((R, HD), F32))
            peers(n, lambda p: ctx_copy(out.at[p], res.at[me], ss2.at[p], rs2.at[me], p).start())
            res[me] = out[me]

        owning(owners, take)

    def await_states(out, res, ss2, rs2):
        peers(owners, lambda o: ctx_copy(out.at[0], res.at[o], ss2.at[0], rs2.at[o], o).wait_recv())

    def state_of(res, h):
        return res[pl.ds(h * per, per)].reshape(HD, HD)

    def local_state(i, c):
        h = lax.rem(i + me, heads)
        cols = cols_of(h)
        conv(1, h)
        conv(2, h)
        ks = (kc[:, cols].astype(F32) * shrink_of(h)).astype(BF16)
        hand_out(dot_tn(ks, vc[:, cols]), h, fs, fr, f1_s, f1_r)
        return c

    lax.fori_loop(0, heads, local_state, 0)

    def inner(h, c):
        cols = cols_of(h)
        conv(0, h)
        q0, q1 = qc[:HALF, cols], qc[HALF:, cols]
        a0 = (dot_nt(q0, kc[:HALF, cols]) * w0[h]).astype(BF16)
        a1 = (dot_nt(q1, kc[:, cols]) * w1[h]).astype(BF16)
        p0[h] = a0
        p1[h] = a1
        att[:HALF, cols] = dot_nn(a0, vc[:HALF, cols])
        att[HALF:, cols] = dot_nn(a1, vc[:, cols])
        return c

    lax.fori_loop(0, heads // 2, inner, 0)

    def clos_in():
        peers(n, lambda s: clos_copy(me, s).wait_recv())

    owning(owners, clos_in)
    scan_slices(False, fs, f1_s, fr, f1_r, fo, fi, f2_s, f2_r)
    lax.fori_loop(heads // 2, heads, inner, 0)
    await_states(fo, fi, f2_s, f2_r)

    accs[...] = jnp.zeros_like(accs)
    acci[...] = jnp.zeros_like(acci)

    def outer(h, c):
        cols = cols_of(h)
        a = att[:, cols] + dot_nn(qc[:, cols], state_of(fi, h)) * jnp.exp(colb[h])
        att[:, cols] = a
        accs[...] += a * a
        acci[...] += gb[:, cols].astype(F32) * gain_ref[0:1, cols] * a
        return c

    lax.fori_loop(0, heads, outer, 0)
    hs_tx[0:1, :] = jnp.sum(accs[...].T, axis=0, keepdims=True)
    hs_tx[1:2, :] = jnp.sum(acci[...].T, axis=0, keepdims=True)

    def sums_copy(p, source):
        return head_copy(hs_tx, hs_rx.at[source], hs_s.at[p], hs_r.at[source], p)

    for d in range(1, m):
        sums_copy(lax.rem(hme + d, m), hme).start()
    hs_rx[hme] = hs_tx[...]
    for d in range(1, m):
        sums_copy(hme, lax.rem(hme + d, m)).wait_recv()
    sums = hs_rx[0]
    for d in range(1, m):
        sums = sums + hs_rx[d]
    inverse = lax.rsqrt(sums[0:1, :] / total + EPS)
    coef = inverse * inverse * (sums[1:2, :] / total)
    both = jnp.concatenate([inverse, coef, jnp.zeros((6, GROUP), F32)], axis=0).T
    invb[...] = jnp.broadcast_to(both[:, 0:1], (GROUP, HD))
    coefb[...] = jnp.broadcast_to(both[:, 1:2], (GROUP, HD))

    def norm(i, c):
        h = lax.rem(i + me, heads)
        cols = cols_of(h)
        a = att[:, cols]
        inv = invb[...]
        normed = a * inv
        gain = gain_ref[0:1, cols]
        gw = gb[:, cols].astype(F32)
        mixb[:, cols] = (normed * gain).astype(BF16)
        tap[heads + h, 4:5, :] = jnp.sum(gw * normed, axis=0, keepdims=True)
        o = (inv * (gw * gain - a * coefb[...])).astype(BF16)
        og[:, cols] = o
        qs = (qc[:, cols].astype(F32) * jnp.exp(colb[h])).astype(BF16)
        hand_out(dot_tn(qs, o), h, bs, br, b1_s, b1_r)
        return c

    lax.fori_loop(0, heads, norm, 0)
    mix_out = pltpu.make_async_copy(mixb, mix_hbm, loc.at[4])
    mix_out.start()

    def back(h, c):
        cols = cols_of(h)
        o0, o1 = og[:HALF, cols], og[HALF:, cols]
        s0 = (dot_nt(o0, vc[:HALF, cols]) * w0[h]).astype(BF16)
        s1 = (dot_nt(o1, vc[:, cols]) * w1[h]).astype(BF16)
        through = dot_nt(og[:, cols], state_of(fi, h)) * jnp.exp(colb[h])
        cg[0, :HALF, cols] = dot_nn(s0, kc[:HALF, cols]) + through[:HALF]
        cg[0, HALF:GROUP, cols] = dot_nn(s1, kc[:, cols]) + through[HALF:]
        kk = dot_tn(s1, qc[HALF:, cols])
        cg[1, :HALF, cols] = kk[:HALF] + dot_tn(s0, qc[:HALF, cols])
        cg[1, HALF:GROUP, cols] = kk[HALF:]
        vv = dot_tn(p1[h], o1)
        cg[2, :HALF, cols] = vv[:HALF] + dot_tn(p0[h], o0)
        cg[2, HALF:GROUP, cols] = vv[HALF:]
        return c

    lax.fori_loop(0, heads // 2, back, 0)
    scan_slices(True, bs, b1_s, br, b1_r, bo, bi, b2_s, b2_r)
    lax.fori_loop(heads // 2, heads, back, 0)

    def edge(c):
        return ctx_copy(
            cg.at[c, pl.ds(0, 8), :], cg.at[c, pl.ds(GROUP, 8), :],
            eh_s.at[c], eh_r.at[c], lax.rem(me + n - 1, n),
        )

    @pl.when(me == n - 1)
    def _():
        cg[:, pl.ds(GROUP, 8), :] = jnp.zeros((3, 8, width), F32)

    @pl.when(me > 0)
    def _():
        edge(0).start()

    def taps(c, h):
        cols = cols_of(h)
        part = cg[c, :GROUP, cols]
        for j in range(TAPS):
            r = c * TAPS + j
            tap[(r // 8) * heads + h, r % 8 : r % 8 + 1, :] = jnp.sum(
                part * xf[c, pl.ds(PAD - j, GROUP), cols], axis=0, keepdims=True
            )

    def q_taps(h, c):
        taps(0, h)
        return c

    lax.fori_loop(0, heads, q_taps, 0)
    await_states(bo, bi, b2_s, b2_r)

    def late(h, c):
        cols = cols_of(h)
        state = state_of(bi, h)
        sh = shrink_of(h)
        cg[1, :GROUP, cols] += dot_nt(vc[:, cols], state) * sh
        cg[2, :GROUP, cols] += dot_nn(kc[:, cols], state) * sh
        return c

    lax.fori_loop(0, heads, late, 0)

    @pl.when(me > 0)
    def _():
        edge(1).start()
        edge(2).start()

    def kv_taps(h, c):
        taps(1, h)
        taps(2, h)
        return c

    lax.fori_loop(0, heads, kv_taps, 0)

    def tap_copy(o, source):
        return ctx_copy(tap.at[o], tapr.at[source], t1_s.at[o], t1_r.at[source], o)

    peers(tiles, lambda o: tap_copy(o, me).start())

    @pl.when(me < n - 1)
    def _():
        for c in range(3):
            edge(c).wait_recv()

    def unconv(c):
        def one(h, carry):
            cols = cols_of(h)
            y = w_ref[c, 0:1, cols] * cg[c, pl.ds(0, GROUP), cols]
            for j in range(1, TAPS):
                y = y + w_ref[c, j : j + 1, cols] * cg[c, pl.ds(j, GROUP), cols]
            outb[c, :, cols] = y.astype(BF16)
            return carry

        lax.fori_loop(0, heads, one, 0)

    outs = [
        pltpu.make_async_copy(outb.at[c], dst, loc.at[5 + c])
        for c, dst in enumerate((qg_hbm, kg_hbm, vg_hbm))
    ]
    unconv(0)
    outs[0].start()

    def sum_copy(p, source):
        return ctx_copy(tsum, tapo.at[source], t2_s.at[p], t2_r.at[source], p)

    def own_sum():
        tapr[me] = tap[me]
        peers(n, lambda s: tap_copy(0, s).wait_recv())
        tsum[...] = lax.fori_loop(0, n, lambda s, a: a + tapr[s], jnp.zeros((8, HD), F32))
        tapo[me] = tsum[...]
        peers(n, lambda p: sum_copy(p, me).start())

    owning(tiles, own_sum)
    unconv(1)
    outs[1].start()
    unconv(2)
    outs[2].start()
    peers(tiles, lambda o: sum_copy(0, o).wait_recv())
    for h in range(heads):
        cols = slice(h * HD, (h + 1) * HD)
        low, high = tapo[h], tapo[heads + h]
        cgrad_ref[0, :, cols] = low[0:4]
        cgrad_ref[1, :, cols] = low[4:8]
        cgrad_ref[2, :, cols] = high[0:4]
        ggrad_ref[0:1, cols] = high[4:5]

    @pl.when(me < n - 1)
    def _():
        for c in range(3):
            halo(c).wait_send()

    @pl.when(me > 0)
    def _():
        for c in range(3):
            edge(c).wait_send()

    def sent_to_owner(o):
        clos_copy(o, me).wait_send()
        slice_copy(fs, fr, f1_s, f1_r, o, me).wait_send()
        slice_copy(bs, br, b1_s, b1_r, o, me).wait_send()

    peers(owners, sent_to_owner)

    def sent_states():
        def one(p):
            ctx_copy(fo.at[p], fi.at[me], f2_s.at[p], f2_r.at[me], p).wait_send()
            ctx_copy(bo.at[p], bi.at[me], b2_s.at[p], b2_r.at[me], p).wait_send()

        peers(n, one)

    owning(owners, sent_states)
    for d in range(1, m):
        sums_copy(lax.rem(hme + d, m), hme).wait_send()
    peers(tiles, lambda o: tap_copy(o, me).wait_send())
    owning(tiles, lambda: peers(n, lambda p: sum_copy(p, me).wait_send()))
    mix_out.wait()
    for cp in outs:
        cp.wait()


def body(n, m, query_rows, key_rows, value_rows, log_gate, conv_weight, norm_gain, mixed_grad):
    tok_here, width = query_rows.shape
    assert tok_here == GROUP
    heads = width // HD
    owners = min(n, width // 16)
    per = owners // heads
    R = HD // per
    tiles = 2 * heads
    assert tiles <= n
    if heads < 8:
        log_gate = jnp.pad(log_gate, ((0, 8 - heads), (0, 0)))
    any_ = pl.BlockSpec(memory_space=pl.ANY)
    vm = pl.BlockSpec(memory_space=pltpu.VMEM)
    V = pltpu.VMEM
    S = pltpu.SemaphoreType.DMA
    rows = jax.ShapeDtypeStruct((GROUP, width), BF16)
    result = pl.pallas_call(
        functools.partial(kernel, n, m, heads, owners),
        out_shape=(
            rows, rows, rows, rows,
            jax.ShapeDtypeStruct((3, TAPS, width), F32),
            jax.ShapeDtypeStruct((1, width), F32),
        ),
        in_specs=[any_] * 4 + [vm] * 3,
        out_specs=(any_, any_, any_, any_, vm, vm),
        scratch_shapes=[
            V((3, PAD + GROUP, width), BF16),
            V((3, PAD + GROUP, width), F32),
            V((GROUP, width), BF16),
            V((GROUP, width), BF16),
            V((GROUP, width), BF16),
            V((GROUP, width), BF16),
            V((GROUP, width), F32),
            V((GROUP, width), BF16),
            V((GROUP, width), BF16),
            V((3, GROUP, width), BF16),
            V((3, GROUP + 8, width), F32),
            V((heads, HALF, HALF), F32),
            V((heads, HALF, GROUP), F32),
            V((heads, HALF, HALF), BF16),
            V((heads, HALF, GROUP), BF16),
            V((heads, GROUP, HD), F32),
            V((heads, 8, GROUP), F32),
            V((heads, 8, HD), F32),
            V((n, 8, HD), F32),
            V((owners, R, HD), BF16),
            V((n, R, HD), BF16),
            V((n, R, HD), BF16),
            V((owners, R, HD), BF16),
            V((owners, R, HD), BF16),
            V((n, R, HD), BF16),
            V((n, R, HD), BF16),
            V((owners, R, HD), BF16),
            V((GROUP, HD), F32),
            V((GROUP, HD), F32),
            V((GROUP, HD), F32),
            V((GROUP, HD), F32),
            V((8, GROUP), F32),
            V((m, 8, GROUP), F32),
            V((tiles, 8, HD), F32),
            V((n, 8, HD), F32),
            V((8, HD), F32),
            V((tiles, 8, HD), F32),
            S((8,)), S((3,)), S((3,)), S((n,)), S((n,)),
            S((n,)), S((n,)), S((n,)), S((n,)),
            S((n,)), S((n,)), S((n,)), S((n,)),
            S((m,)), S((m,)), S((3,)), S((3,)),
            S((n,)), S((n,)), S((n,)), S((n,)),
        ],
        compiler_params=pltpu.CompilerParams(
            collective_id=0, has_side_effects=True, vmem_limit_bytes=60 * 1024 * 1024
        ),
    )(
        query_rows, key_rows, value_rows, mixed_grad,
        log_gate, conv_weight, norm_gain.reshape(1, width),
    )
    return (*result[:5], result[5].reshape(width))


def solution(mesh):
    n, m = mesh.shape["ctx"], mesh.shape["head"]
    rows = P("ctx", "head")
    return jax.shard_map(
        functools.partial(body, n, m),
        mesh=mesh,
        in_specs=(rows, rows, rows, P("head", "ctx"), P(None, None, "head"), P("head"), rows),
        out_specs=(rows, rows, rows, rows, P(None, None, "head"), P("head")),
        check_vma=False,
    )
```

```python
import functools

import jax
import jax.numpy as jnp
from jax import lax
from jax.experimental import pallas as pl
from jax.experimental.pallas import tpu as pltpu
from jax.sharding import PartitionSpec as P

HD = 128
TAPS = 4
GROUP = 512
HALF = GROUP // 2
UNROLL = 8
PAD = 16
EPS = 1e-05
MESH = pl.DeviceIdType.MESH
F32 = jnp.float32
BF16 = jnp.bfloat16


def dot_nn(a, b):
    return lax.dot_general(a, b, (((1,), (0,)), ((), ())), preferred_element_type=F32)


def dot_nt(a, b):
    return lax.dot_general(a, b, (((1,), (1,)), ((), ())), preferred_element_type=F32)


def dot_tn(a, b):
    return lax.dot_general(a, b, (((0,), (0,)), ((), ())), preferred_element_type=F32)


def kernel(
    n, m, heads, owners,
    q_hbm, k_hbm, v_hbm, g_hbm, lg_ref, w_ref, gain_ref,
    mix_hbm, qg_hbm, kg_hbm, vg_hbm, cgrad_ref, ggrad_ref,
    ext, xf, qc, kc, vc, gb, att, og, mixb, outb, cg,
    w0, w1, p0, p1, colb, rowb, closb, closr,
    fs, fr, fo, fi, bs, br, bo, bi,
    accs, acci, invb, coefb, hs_tx, hs_rx,
    tap, tapr, tsum, tapo,
    loc, ha_s, ha_r, cl_s, cl_r,
    f1_s, f1_r, f2_s, f2_r, b1_s, b1_r, b2_s, b2_r,
    hs_s, hs_r, eh_s, eh_r, t1_s, t1_r, t2_s, t2_r,
):
    me = lax.axis_index("ctx")
    hme = lax.axis_index("head")
    per = owners // heads
    R = HD // per
    tiles = 2 * heads
    width = heads * HD
    total = width * m
    convs = (qc, kc, vc)

    def ctx_copy(src, dst, ss, rs, p):
        return pltpu.make_async_remote_copy(
            src_ref=src, dst_ref=dst, send_sem=ss, recv_sem=rs,
            device_id={"ctx": p}, device_id_type=MESH,
        )

    def head_copy(src, dst, ss, rs, p):
        return pltpu.make_async_remote_copy(
            src_ref=src, dst_ref=dst, send_sem=ss, recv_sem=rs,
            device_id={"head": p}, device_id_type=MESH,
        )

    def peers(count, fn):
        def one(d, c):
            p = lax.rem(me + d, n)
            if count == n:
                fn(p)
            else:
                pl.when(p < count)(lambda: fn(p))
            return c

        lax.fori_loop(1, n, one, 0)

    def owning(count, fn):
        if count == n:
            fn()
        else:
            pl.when(me < count)(fn)

    def cols_of(h):
        if isinstance(h, int):
            return pl.ds(h * HD, HD)
        return pl.ds(pl.multiple_of(h * HD, HD), HD)

    def over(lo, hi, fn):
        k = min(UNROLL, hi - lo)
        if k == hi - lo:
            for h in range(lo, hi):
                fn(h, 0)
        else:

            def some(i, c):
                for u in range(k):
                    fn(lo + i * k + u, 0)
                return c

            lax.fori_loop(0, (hi - lo) // k, some, 0)

    ins = [
        pltpu.make_async_copy(src, ext.at[c, pl.ds(PAD, GROUP), :], loc.at[c])
        for c, src in enumerate((q_hbm, k_hbm, v_hbm))
    ]
    ins.append(pltpu.make_async_copy(g_hbm, gb, loc.at[3]))
    for cp in ins:
        cp.start()

    barrier = pltpu.get_barrier_semaphore()

    def greet(p):
        pl.semaphore_signal(barrier, inc=1, device_id={"ctx": p}, device_id_type=MESH)

    peers(n, greet)
    for d in range(1, m):
        pl.semaphore_signal(
            barrier, inc=1, device_id={"head": lax.rem(hme + d, m)}, device_id_type=MESH
        )

    run = lg_ref[...]
    lane = lax.broadcasted_iota(jnp.int32, run.shape, 1)
    d = 1
    while d < GROUP:
        run = run + jnp.where(lane >= d, pltpu.roll(run, d, 1), 0.0)
        d *= 2
    run_t = run.T
    for h in range(heads):
        colb[h] = jnp.broadcast_to(run_t[:, h : h + 1], (GROUP, HD))
        rowb[h] = jnp.broadcast_to(run[h : h + 1, :], (8, GROUP))
        closb[h] = jnp.broadcast_to(run[h : h + 1, GROUP - 1 : GROUP], (8, HD))

    tap[...] = jnp.zeros_like(tap)
    hs_tx[...] = jnp.zeros_like(hs_tx)

    for cp in ins:
        cp.wait()
    pl.semaphore_wait(barrier, n - 1 + m - 1)

    def halo(c):
        return ctx_copy(
            ext.at[c, pl.ds(GROUP, PAD), :], ext.at[c, pl.ds(0, PAD), :],
            ha_s.at[c], ha_r.at[c], lax.rem(me + 1, n),
        )

    @pl.when(me < n - 1)
    def _():
        for c in (1, 2, 0):
            halo(c).start()

    @pl.when(me == 0)
    def _():
        ext[:, pl.ds(0, PAD), :] = jnp.zeros((3, PAD, width), BF16)

    def clos_copy(p, source):
        return ctx_copy(closb.at[p // per], closr.at[source], cl_s.at[p], cl_r.at[source], p)

    peers(owners, lambda p: clos_copy(p, me).start())

    def own_clos():
        closr[me] = closb[me // per]

    owning(owners, own_clos)

    def decay(h, c):
        col = colb[h]
        row = rowb[h][0:1, :]
        top = jnp.concatenate([col[:HALF]] * 2, axis=1)
        low = jnp.concatenate([col[HALF:]] * 2, axis=1)
        keep = lax.broadcasted_iota(jnp.int32, (HALF, HALF), 0) >= lax.broadcasted_iota(
            jnp.int32, (HALF, HALF), 1
        )
        w0[h] = jnp.where(keep, jnp.exp(jnp.minimum(top - row[:, :HALF], 0.0)), 0.0)
        w1[h, :, :HALF] = jnp.exp(jnp.minimum(low - row[:, :HALF], 0.0))
        w1[h, :, HALF:] = jnp.where(keep, jnp.exp(jnp.minimum(low - row[:, HALF:], 0.0)), 0.0)
        return c

    over(0, heads, decay)

    @pl.when(me > 0)
    def _():
        for c in range(3):
            halo(c).wait_recv()

    def conv(c, h):
        cols = cols_of(h)
        xf[c, :, cols] = ext[c, :, cols].astype(F32)
        y = w_ref[c, 0:1, cols] * xf[c, pl.ds(PAD, GROUP), cols]
        for j in range(1, TAPS):
            y = y + w_ref[c, j : j + 1, cols] * xf[c, pl.ds(PAD - j, GROUP), cols]
        convs[c][:, cols] = y.astype(BF16)

    def shrink_of(h):
        return jnp.exp(closb[h][0:1, :] - colb[h])

    def slice_copy(src, dst, ss, rs, o, source):
        return ctx_copy(src.at[o], dst.at[source], ss.at[o], rs.at[source], o)

    def keep_slices(state, h, src):
        state = state.astype(BF16)
        for i in range(per):
            src[h * per + i] = state[i * R : (i + 1) * R]

    def hand_out(lo, hi, src, dst, ss, rs):
        span = (hi - lo) * per

        def one(d, c):
            o = lo * per + lax.rem(d + me, span)

            @pl.when(o != me)
            def _():
                slice_copy(src, dst, ss, rs, o, me).start()

            @pl.when(o == me)
            def _():
                dst[me] = src[me]

            return c

        lax.fori_loop(0, span, one, 0)

    def scan_slices(backwards, src, ss, got, rs, out, res, ss2, rs2):
        def take():
            peers(n, lambda s: slice_copy(src, got, ss, rs, 0, s).wait_recv())

            def step(i, state):
                b = n - 1 - i if backwards else i
                out[b] = state.astype(BF16)
                return jnp.exp(closr[b][0:1, :]) * state + got[b].astype(F32)

            lax.fori_loop(0, n, step, jnp.zeros((R, HD), F32))
            peers(n, lambda p: ctx_copy(out.at[p], res.at[me], ss2.at[p], rs2.at[me], p).start())
            res[me] = out[me]

        owning(owners, take)

    def await_states(out, res, ss2, rs2):
        peers(owners, lambda o: ctx_copy(out.at[0], res.at[o], ss2.at[0], rs2.at[o], o).wait_recv())

    def state_of(res, h):
        return res[pl.ds(h * per, per)].reshape(HD, HD)

    def local_state(h, c):
        cols = cols_of(h)
        conv(1, h)
        conv(2, h)
        ks = (kc[:, cols].astype(F32) * shrink_of(h)).astype(BF16)
        keep_slices(dot_tn(ks, vc[:, cols]), h, fs)
        return c

    mid = heads // 2
    over(0, mid, local_state)
    hand_out(0, mid, fs, fr, f1_s, f1_r)
    over(mid, heads, local_state)
    hand_out(mid, heads, fs, fr, f1_s, f1_r)

    def inner(h, c):
        cols = cols_of(h)
        conv(0, h)
        q0, q1 = qc[:HALF, cols], qc[HALF:, cols]
        a0 = (dot_nt(q0, kc[:HALF, cols]) * w0[h]).astype(BF16)
        a1 = (dot_nt(q1, kc[:, cols]) * w1[h]).astype(BF16)
        p0[h] = a0
        p1[h] = a1
        att[:HALF, cols] = dot_nn(a0, vc[:HALF, cols])
        att[HALF:, cols] = dot_nn(a1, vc[:, cols])
        return c

    over(0, mid, inner)

    def clos_in():
        peers(n, lambda s: clos_copy(me, s).wait_recv())

    owning(owners, clos_in)
    scan_slices(False, fs, f1_s, fr, f1_r, fo, fi, f2_s, f2_r)
    over(mid, heads, inner)
    await_states(fo, fi, f2_s, f2_r)

    accs[...] = jnp.zeros_like(accs)
    acci[...] = jnp.zeros_like(acci)

    def outer(h, c):
        cols = cols_of(h)
        a = att[:, cols] + dot_nn(qc[:, cols], state_of(fi, h)) * jnp.exp(colb[h])
        att[:, cols] = a
        accs[...] += a * a
        acci[...] += gb[:, cols].astype(F32) * gain_ref[0:1, cols] * a
        return c

    over(0, heads, outer)
    hs_tx[0:1, :] = jnp.sum(accs[...].T, axis=0, keepdims=True)
    hs_tx[1:2, :] = jnp.sum(acci[...].T, axis=0, keepdims=True)

    def sums_copy(p, source):
        return head_copy(hs_tx, hs_rx.at[source], hs_s.at[p], hs_r.at[source], p)

    for d in range(1, m):
        sums_copy(lax.rem(hme + d, m), hme).start()
    hs_rx[hme] = hs_tx[...]
    for d in range(1, m):
        sums_copy(hme, lax.rem(hme + d, m)).wait_recv()
    sums = hs_rx[0]
    for d in range(1, m):
        sums = sums + hs_rx[d]
    inverse = lax.rsqrt(sums[0:1, :] / total + EPS)
    coef = inverse * inverse * (sums[1:2, :] / total)
    both = jnp.concatenate([inverse, coef, jnp.zeros((6, GROUP), F32)], axis=0).T
    invb[...] = jnp.broadcast_to(both[:, 0:1], (GROUP, HD))
    coefb[...] = jnp.broadcast_to(both[:, 1:2], (GROUP, HD))

    def norm(h, c):
        cols = cols_of(h)
        a = att[:, cols]
        inv = invb[...]
        normed = a * inv
        gain = gain_ref[0:1, cols]
        gw = gb[:, cols].astype(F32)
        mixb[:, cols] = (normed * gain).astype(BF16)
        tap[heads + h, 4:5, :] = jnp.sum(gw * normed, axis=0, keepdims=True)
        o = (inv * (gw * gain - a * coefb[...])).astype(BF16)
        og[:, cols] = o
        qs = (qc[:, cols].astype(F32) * jnp.exp(colb[h])).astype(BF16)
        keep_slices(dot_tn(qs, o), h, bs)
        return c

    over(0, mid, norm)
    hand_out(0, mid, bs, br, b1_s, b1_r)
    over(mid, heads, norm)
    hand_out(mid, heads, bs, br, b1_s, b1_r)
    mix_out = pltpu.make_async_copy(mixb, mix_hbm, loc.at[4])
    mix_out.start()

    def back(h, c):
        cols = cols_of(h)
        o0, o1 = og[:HALF, cols], og[HALF:, cols]
        s0 = (dot_nt(o0, vc[:HALF, cols]) * w0[h]).astype(BF16)
        s1 = (dot_nt(o1, vc[:, cols]) * w1[h]).astype(BF16)
        through = dot_nt(og[:, cols], state_of(fi, h)) * jnp.exp(colb[h])
        cg[0, :HALF, cols] = dot_nn(s0, kc[:HALF, cols]) + through[:HALF]
        cg[0, HALF:GROUP, cols] = dot_nn(s1, kc[:, cols]) + through[HALF:]
        kk = dot_tn(s1, qc[HALF:, cols])
        cg[1, :HALF, cols] = kk[:HALF] + dot_tn(s0, qc[:HALF, cols])
        cg[1, HALF:GROUP, cols] = kk[HALF:]
        vv = dot_tn(p1[h], o1)
        cg[2, :HALF, cols] = vv[:HALF] + dot_tn(p0[h], o0)
        cg[2, HALF:GROUP, cols] = vv[HALF:]
        return c

    over(0, mid, back)
    scan_slices(True, bs, b1_s, br, b1_r, bo, bi, b2_s, b2_r)
    over(mid, heads, back)

    def edge(c):
        return ctx_copy(
            cg.at[c, pl.ds(0, 8), :], cg.at[c, pl.ds(GROUP, 8), :],
            eh_s.at[c], eh_r.at[c], lax.rem(me + n - 1, n),
        )

    @pl.when(me == n - 1)
    def _():
        cg[:, pl.ds(GROUP, 8), :] = jnp.zeros((3, 8, width), F32)

    @pl.when(me > 0)
    def _():
        edge(0).start()

    def taps(c, h):
        cols = cols_of(h)
        part = cg[c, :GROUP, cols]
        for j in range(TAPS):
            r = c * TAPS + j
            tap[(r // 8) * heads + h, r % 8 : r % 8 + 1, :] = jnp.sum(
                part * xf[c, pl.ds(PAD - j, GROUP), cols], axis=0, keepdims=True
            )

    def q_taps(h, c):
        taps(0, h)
        return c

    over(0, heads, q_taps)
    await_states(bo, bi, b2_s, b2_r)

    def late(h, c):
        cols = cols_of(h)
        state = state_of(bi, h)
        sh = shrink_of(h)
        cg[1, :GROUP, cols] += dot_nt(vc[:, cols], state) * sh
        cg[2, :GROUP, cols] += dot_nn(kc[:, cols], state) * sh
        return c

    over(0, heads, late)

    @pl.when(me > 0)
    def _():
        edge(1).start()
        edge(2).start()

    def kv_taps(h, c):
        taps(1, h)
        taps(2, h)
        return c

    over(0, heads, kv_taps)

    def tap_copy(o, source):
        return ctx_copy(tap.at[o], tapr.at[source], t1_s.at[o], t1_r.at[source], o)

    peers(tiles, lambda o: tap_copy(o, me).start())

    @pl.when(me < n - 1)
    def _():
        for c in range(3):
            edge(c).wait_recv()

    def unconv(c):
        def one(h, carry):
            cols = cols_of(h)
            y = w_ref[c, 0:1, cols] * cg[c, pl.ds(0, GROUP), cols]
            for j in range(1, TAPS):
                y = y + w_ref[c, j : j + 1, cols] * cg[c, pl.ds(j, GROUP), cols]
            outb[c, :, cols] = y.astype(BF16)
            return carry

        over(0, heads, one)

    outs = [
        pltpu.make_async_copy(outb.at[c], dst, loc.at[5 + c])
        for c, dst in enumerate((qg_hbm, kg_hbm, vg_hbm))
    ]
    unconv(0)
    outs[0].start()

    def sum_copy(p, source):
        return ctx_copy(tsum, tapo.at[source], t2_s.at[p], t2_r.at[source], p)

    def own_sum():
        tapr[me] = tap[me]
        peers(n, lambda s: tap_copy(0, s).wait_recv())
        tsum[...] = lax.fori_loop(0, n, lambda s, a: a + tapr[s], jnp.zeros((8, HD), F32))
        tapo[me] = tsum[...]
        peers(n, lambda p: sum_copy(p, me).start())

    owning(tiles, own_sum)
    unconv(1)
    outs[1].start()
    unconv(2)
    outs[2].start()
    peers(tiles, lambda o: sum_copy(0, o).wait_recv())
    for h in range(heads):
        cols = slice(h * HD, (h + 1) * HD)
        low, high = tapo[h], tapo[heads + h]
        cgrad_ref[0, :, cols] = low[0:4]
        cgrad_ref[1, :, cols] = low[4:8]
        cgrad_ref[2, :, cols] = high[0:4]
        ggrad_ref[0:1, cols] = high[4:5]

    @pl.when(me < n - 1)
    def _():
        for c in range(3):
            halo(c).wait_send()

    @pl.when(me > 0)
    def _():
        for c in range(3):
            edge(c).wait_send()

    def sent_to_owner(o):
        clos_copy(o, me).wait_send()
        slice_copy(fs, fr, f1_s, f1_r, o, me).wait_send()
        slice_copy(bs, br, b1_s, b1_r, o, me).wait_send()

    peers(owners, sent_to_owner)

    def sent_states():
        def one(p):
            ctx_copy(fo.at[p], fi.at[me], f2_s.at[p], f2_r.at[me], p).wait_send()
            ctx_copy(bo.at[p], bi.at[me], b2_s.at[p], b2_r.at[me], p).wait_send()

        peers(n, one)

    owning(owners, sent_states)
    for d in range(1, m):
        sums_copy(lax.rem(hme + d, m), hme).wait_send()
    peers(tiles, lambda o: tap_copy(o, me).wait_send())
    owning(tiles, lambda: peers(n, lambda p: sum_copy(p, me).wait_send()))
    mix_out.wait()
    for cp in outs:
        cp.wait()


PIECES = 4


def hand_on(*refs):
    count = (len(refs) - 3) // 2
    srcs, dsts = refs[:count], refs[count : 2 * count]
    stage, got, put = refs[-3:]
    step = GROUP // PIECES
    loads, stores = [], []
    for j in range(PIECES):
        part = pl.ds(j * step, step)
        for i in range(4):
            k = i * PIECES + j
            loads.append(
                pltpu.make_async_copy(srcs[i].at[part, :], stage.at[i, part, :], got.at[k])
            )
            stores.append(
                pltpu.make_async_copy(stage.at[i, part, :], dsts[i].at[part, :], put.at[k])
            )
    for cp in loads:
        cp.start()
    for i in range(4, count):
        dsts[i][...] = srcs[i][...]
    for cp, out in zip(loads, stores):
        cp.wait()
        out.start()
    for out in stores:
        out.wait()


def body(n, m, query_rows, key_rows, value_rows, log_gate, conv_weight, norm_gain, mixed_grad):
    tok_here, width = query_rows.shape
    assert tok_here == GROUP
    heads = width // HD
    owners = min(n, width // 16)
    per = owners // heads
    R = HD // per
    tiles = 2 * heads
    assert tiles <= n
    if heads < 8:
        log_gate = jnp.pad(log_gate, ((0, 8 - heads), (0, 0)))
    any_ = pl.BlockSpec(memory_space=pl.ANY)
    vm = pl.BlockSpec(memory_space=pltpu.VMEM)
    V = pltpu.VMEM
    S = pltpu.SemaphoreType.DMA
    rows = jax.ShapeDtypeStruct((GROUP, width), BF16)
    result = pl.pallas_call(
        functools.partial(kernel, n, m, heads, owners),
        out_shape=(
            rows, rows, rows, rows,
            jax.ShapeDtypeStruct((3, TAPS, width), F32),
            jax.ShapeDtypeStruct((1, width), F32),
        ),
        in_specs=[any_] * 4 + [vm] * 3,
        out_specs=(any_, any_, any_, any_, vm, vm),
        scratch_shapes=[
            V((3, PAD + GROUP, width), BF16),
            V((3, PAD + GROUP, width), F32),
            V((GROUP, width), BF16),
            V((GROUP, width), BF16),
            V((GROUP, width), BF16),
            V((GROUP, width), BF16),
            V((GROUP, width), F32),
            V((GROUP, width), BF16),
            V((GROUP, width), BF16),
            V((3, GROUP, width), BF16),
            V((3, GROUP + 8, width), F32),
            V((heads, HALF, HALF), F32),
            V((heads, HALF, GROUP), F32),
            V((heads, HALF, HALF), BF16),
            V((heads, HALF, GROUP), BF16),
            V((heads, GROUP, HD), F32),
            V((heads, 8, GROUP), F32),
            V((heads, 8, HD), F32),
            V((n, 8, HD), F32),
            V((owners, R, HD), BF16),
            V((n, R, HD), BF16),
            V((n, R, HD), BF16),
            V((owners, R, HD), BF16),
            V((owners, R, HD), BF16),
            V((n, R, HD), BF16),
            V((n, R, HD), BF16),
            V((owners, R, HD), BF16),
            V((GROUP, HD), F32),
            V((GROUP, HD), F32),
            V((GROUP, HD), F32),
            V((GROUP, HD), F32),
            V((8, GROUP), F32),
            V((m, 8, GROUP), F32),
            V((tiles, 8, HD), F32),
            V((n, 8, HD), F32),
            V((8, HD), F32),
            V((tiles, 8, HD), F32),
            S((8,)), S((3,)), S((3,)), S((n,)), S((n,)),
            S((n,)), S((n,)), S((n,)), S((n,)),
            S((n,)), S((n,)), S((n,)), S((n,)),
            S((m,)), S((m,)), S((3,)), S((3,)),
            S((n,)), S((n,)), S((n,)), S((n,)),
        ],
        compiler_params=pltpu.CompilerParams(
            collective_id=0, has_side_effects=True, vmem_limit_bytes=60 * 1024 * 1024
        ),
    )(
        query_rows, key_rows, value_rows, mixed_grad,
        log_gate, conv_weight, norm_gain.reshape(1, width),
    )
    specs = [any_] * 4 + [vm] * 2
    result = pl.pallas_call(
        hand_on,
        out_shape=tuple(jax.ShapeDtypeStruct(r.shape, r.dtype) for r in result),
        in_specs=specs,
        out_specs=tuple(specs),
        scratch_shapes=[V((4, GROUP, width), BF16), S((4 * PIECES,)), S((4 * PIECES,))],
    )(*result)
    return (*result[:5], result[5].reshape(width))


def solution(mesh):
    n, m = mesh.shape["ctx"], mesh.shape["head"]
    rows = P("ctx", "head")
    return jax.shard_map(
        functools.partial(body, n, m),
        mesh=mesh,
        in_specs=(rows, rows, rows, P("head", "ctx"), P(None, None, "head"), P("head"), rows),
        out_specs=(rows, rows, rows, rows, P(None, None, "head"), P("head")),
        check_vma=False,
    )
```

```python
import functools

import jax
import jax.numpy as jnp
from jax import lax
from jax.experimental import pallas as pl
from jax.experimental.pallas import tpu as pltpu
from jax.sharding import PartitionSpec as P

HD = 128
TAPS = 4
GROUP = 512
HALF = GROUP // 2
UNROLL = 8
PAD = 16
EPS = 1e-05
MESH = pl.DeviceIdType.MESH
F32 = jnp.float32
BF16 = jnp.bfloat16


def dot_nn(a, b):
    return lax.dot_general(a, b, (((1,), (0,)), ((), ())), preferred_element_type=F32)


def dot_nt(a, b):
    return lax.dot_general(a, b, (((1,), (1,)), ((), ())), preferred_element_type=F32)


def dot_tn(a, b):
    return lax.dot_general(a, b, (((0,), (0,)), ((), ())), preferred_element_type=F32)


def kernel(
    n, m, heads, owners,
    q_hbm, k_hbm, v_hbm, g_hbm, lg_ref, w_ref, gain_ref,
    mix_hbm, qg_hbm, kg_hbm, vg_hbm, cgrad_ref, ggrad_ref,
    ext, xf, qc, kc, vc, gb, att, og, mixb, outb, cg,
    w0, w1, p0, p1, colb, rowb, closb, closr,
    fs, fr, fo, fi, bs, br, bo, bi,
    accs, acci, invb, coefb, hs_tx, hs_rx,
    tap, tapr, tsum, tapo,
    loc, ha_s, ha_r, cl_s, cl_r,
    f1_s, f1_r, f2_s, f2_r, b1_s, b1_r, b2_s, b2_r,
    hs_s, hs_r, eh_s, eh_r, t1_s, t1_r, t2_s, t2_r,
):
    me = lax.axis_index("ctx")
    hme = lax.axis_index("head")
    per = owners // heads
    R = HD // per
    tiles = 2 * heads
    width = heads * HD
    total = width * m
    convs = (qc, kc, vc)

    def ctx_copy(src, dst, ss, rs, p):
        return pltpu.make_async_remote_copy(
            src_ref=src, dst_ref=dst, send_sem=ss, recv_sem=rs,
            device_id={"ctx": p}, device_id_type=MESH,
        )

    def head_copy(src, dst, ss, rs, p):
        return pltpu.make_async_remote_copy(
            src_ref=src, dst_ref=dst, send_sem=ss, recv_sem=rs,
            device_id={"head": p}, device_id_type=MESH,
        )

    def peers(count, fn):
        def one(d, c):
            p = lax.rem(me + d, n)
            if count == n:
                fn(p)
            else:
                pl.when(p < count)(lambda: fn(p))
            return c

        lax.fori_loop(1, n, one, 0)

    def owning(count, fn):
        if count == n:
            fn()
        else:
            pl.when(me < count)(fn)

    def cols_of(h):
        if isinstance(h, int):
            return pl.ds(h * HD, HD)
        return pl.ds(pl.multiple_of(h * HD, HD), HD)

    def over(lo, hi, fn):
        k = min(UNROLL, hi - lo)
        if k == hi - lo:
            for h in range(lo, hi):
                fn(h, 0)
        else:

            def some(i, c):
                for u in range(k):
                    fn(lo + i * k + u, 0)
                return c

            lax.fori_loop(0, (hi - lo) // k, some, 0)

    ins = [
        pltpu.make_async_copy(src, ext.at[c, pl.ds(PAD, GROUP), :], loc.at[c])
        for c, src in enumerate((q_hbm, k_hbm, v_hbm))
    ]
    ins.append(pltpu.make_async_copy(g_hbm, gb, loc.at[3]))
    for cp in ins:
        cp.start()

    barrier = pltpu.get_barrier_semaphore()

    def greet(p):
        pl.semaphore_signal(barrier, inc=1, device_id={"ctx": p}, device_id_type=MESH)

    peers(n, greet)
    for d in range(1, m):
        pl.semaphore_signal(
            barrier, inc=1, device_id={"head": lax.rem(hme + d, m)}, device_id_type=MESH
        )

    run = lg_ref[...]
    lane = lax.broadcasted_iota(jnp.int32, run.shape, 1)
    d = 1
    while d < GROUP:
        run = run + jnp.where(lane >= d, pltpu.roll(run, d, 1), 0.0)
        d *= 2
    run_t = run.T
    for h in range(heads):
        colb[h] = jnp.broadcast_to(run_t[:, h : h + 1], (GROUP, HD))
        rowb[h] = jnp.broadcast_to(run[h : h + 1, :], (8, GROUP))
        closb[h] = jnp.broadcast_to(run[h : h + 1, GROUP - 1 : GROUP], (8, HD))

    tap[...] = jnp.zeros_like(tap)
    hs_tx[...] = jnp.zeros_like(hs_tx)

    for cp in ins:
        cp.wait()
    pl.semaphore_wait(barrier, n - 1 + m - 1)

    def halo(c):
        return ctx_copy(
            ext.at[c, pl.ds(GROUP, PAD), :], ext.at[c, pl.ds(0, PAD), :],
            ha_s.at[c], ha_r.at[c], lax.rem(me + 1, n),
        )

    @pl.when(me < n - 1)
    def _():
        for c in (1, 2, 0):
            halo(c).start()

    @pl.when(me == 0)
    def _():
        ext[:, pl.ds(0, PAD), :] = jnp.zeros((3, PAD, width), BF16)

    def clos_copy(p, source):
        return ctx_copy(closb.at[p // per], closr.at[source], cl_s.at[p], cl_r.at[source], p)

    peers(owners, lambda p: clos_copy(p, me).start())

    def own_clos():
        closr[me] = closb[me // per]

    owning(owners, own_clos)

    def decay(h, c):
        col = colb[h]
        row = rowb[h][0:1, :]
        top = jnp.concatenate([col[:HALF]] * 2, axis=1)
        low = jnp.concatenate([col[HALF:]] * 2, axis=1)
        keep = lax.broadcasted_iota(jnp.int32, (HALF, HALF), 0) >= lax.broadcasted_iota(
            jnp.int32, (HALF, HALF), 1
        )
        w0[h] = jnp.where(keep, jnp.exp(jnp.minimum(top - row[:, :HALF], 0.0)), 0.0)
        w1[h, :, :HALF] = jnp.exp(jnp.minimum(low - row[:, :HALF], 0.0))
        w1[h, :, HALF:] = jnp.where(keep, jnp.exp(jnp.minimum(low - row[:, HALF:], 0.0)), 0.0)
        return c

    over(0, heads // 2, decay)

    @pl.when(me > 0)
    def _():
        for c in range(3):
            halo(c).wait_recv()

    def conv(c, h):
        cols = cols_of(h)
        xf[c, :, cols] = ext[c, :, cols].astype(F32)
        y = w_ref[c, 0:1, cols] * xf[c, pl.ds(PAD, GROUP), cols]
        for j in range(1, TAPS):
            y = y + w_ref[c, j : j + 1, cols] * xf[c, pl.ds(PAD - j, GROUP), cols]
        convs[c][:, cols] = y.astype(BF16)

    def shrink_of(h):
        return jnp.exp(closb[h][0:1, :] - colb[h])

    def slice_copy(src, dst, ss, rs, o, source):
        return ctx_copy(src.at[o], dst.at[source], ss.at[o], rs.at[source], o)

    def keep_slices(state, h, src):
        state = state.astype(BF16)
        for i in range(per):
            src[h * per + i] = state[i * R : (i + 1) * R]

    def hand_out(lo, hi, src, dst, ss, rs):
        span = (hi - lo) * per

        def one(d, c):
            o = lo * per + lax.rem(d + me, span)

            @pl.when(o != me)
            def _():
                slice_copy(src, dst, ss, rs, o, me).start()

            @pl.when(o == me)
            def _():
                dst[me] = src[me]

            return c

        lax.fori_loop(0, span, one, 0)

    def scan_slices(backwards, src, ss, got, rs, out, res, ss2, rs2):
        def take():
            peers(n, lambda s: slice_copy(src, got, ss, rs, 0, s).wait_recv())

            def step(i, state):
                b = n - 1 - i if backwards else i
                out[b] = state.astype(BF16)
                return jnp.exp(closr[b][0:1, :]) * state + got[b].astype(F32)

            lax.fori_loop(0, n, step, jnp.zeros((R, HD), F32))
            peers(n, lambda p: ctx_copy(out.at[p], res.at[me], ss2.at[p], rs2.at[me], p).start())
            res[me] = out[me]

        owning(owners, take)

    def await_states(out, res, ss2, rs2):
        peers(owners, lambda o: ctx_copy(out.at[0], res.at[o], ss2.at[0], rs2.at[o], o).wait_recv())

    def state_of(res, h):
        return res[pl.ds(h * per, per)].reshape(HD, HD)

    def local_state(h, c):
        cols = cols_of(h)
        conv(1, h)
        conv(2, h)
        ks = (kc[:, cols].astype(F32) * shrink_of(h)).astype(BF16)
        keep_slices(dot_tn(ks, vc[:, cols]), h, fs)
        return c

    mid = heads // 2
    over(0, mid, local_state)
    hand_out(0, mid, fs, fr, f1_s, f1_r)
    over(mid, heads, local_state)
    hand_out(mid, heads, fs, fr, f1_s, f1_r)
    over(mid, heads, decay)

    def inner(h, c):
        cols = cols_of(h)
        conv(0, h)
        q0, q1 = qc[:HALF, cols], qc[HALF:, cols]
        a0 = (dot_nt(q0, kc[:HALF, cols]) * w0[h]).astype(BF16)
        a1 = (dot_nt(q1, kc[:, cols]) * w1[h]).astype(BF16)
        p0[h] = a0
        p1[h] = a1
        att[:HALF, cols] = dot_nn(a0, vc[:HALF, cols])
        att[HALF:, cols] = dot_nn(a1, vc[:, cols])
        return c

    over(0, mid, inner)

    def clos_in():
        peers(n, lambda s: clos_copy(me, s).wait_recv())

    owning(owners, clos_in)
    scan_slices(False, fs, f1_s, fr, f1_r, fo, fi, f2_s, f2_r)
    over(mid, heads, inner)
    await_states(fo, fi, f2_s, f2_r)

    accs[...] = jnp.zeros_like(accs)
    acci[...] = jnp.zeros_like(acci)

    def outer(h, c):
        cols = cols_of(h)
        a = att[:, cols] + dot_nn(qc[:, cols], state_of(fi, h)) * jnp.exp(colb[h])
        att[:, cols] = a
        accs[...] += a * a
        acci[...] += gb[:, cols].astype(F32) * gain_ref[0:1, cols] * a
        return c

    over(0, heads, outer)
    hs_tx[0:1, :] = jnp.sum(accs[...].T, axis=0, keepdims=True)
    hs_tx[1:2, :] = jnp.sum(acci[...].T, axis=0, keepdims=True)

    def sums_copy(p, source):
        return head_copy(hs_tx, hs_rx.at[source], hs_s.at[p], hs_r.at[source], p)

    for d in range(1, m):
        sums_copy(lax.rem(hme + d, m), hme).start()
    hs_rx[hme] = hs_tx[...]
    for d in range(1, m):
        sums_copy(hme, lax.rem(hme + d, m)).wait_recv()
    sums = hs_rx[0]
    for d in range(1, m):
        sums = sums + hs_rx[d]
    inverse = lax.rsqrt(sums[0:1, :] / total + EPS)
    coef = inverse * inverse * (sums[1:2, :] / total)
    both = jnp.concatenate([inverse, coef, jnp.zeros((6, GROUP), F32)], axis=0).T
    invb[...] = jnp.broadcast_to(both[:, 0:1], (GROUP, HD))
    coefb[...] = jnp.broadcast_to(both[:, 1:2], (GROUP, HD))

    def norm(h, c):
        cols = cols_of(h)
        a = att[:, cols]
        inv = invb[...]
        normed = a * inv
        gain = gain_ref[0:1, cols]
        gw = gb[:, cols].astype(F32)
        mixb[:, cols] = (normed * gain).astype(BF16)
        tap[heads + h, 4:5, :] = jnp.sum(gw * normed, axis=0, keepdims=True)
        o = (inv * (gw * gain - a * coefb[...])).astype(BF16)
        og[:, cols] = o
        qs = (qc[:, cols].astype(F32) * jnp.exp(colb[h])).astype(BF16)
        keep_slices(dot_tn(qs, o), h, bs)
        return c

    over(0, mid, norm)
    hand_out(0, mid, bs, br, b1_s, b1_r)
    over(mid, heads, norm)
    hand_out(mid, heads, bs, br, b1_s, b1_r)
    mix_out = pltpu.make_async_copy(mixb, mix_hbm, loc.at[4])
    mix_out.start()

    def back(h, c):
        cols = cols_of(h)
        o0, o1 = og[:HALF, cols], og[HALF:, cols]
        s0 = (dot_nt(o0, vc[:HALF, cols]) * w0[h]).astype(BF16)
        s1 = (dot_nt(o1, vc[:, cols]) * w1[h]).astype(BF16)
        through = dot_nt(og[:, cols], state_of(fi, h)) * jnp.exp(colb[h])
        cg[0, :HALF, cols] = dot_nn(s0, kc[:HALF, cols]) + through[:HALF]
        cg[0, HALF:GROUP, cols] = dot_nn(s1, kc[:, cols]) + through[HALF:]
        kk = dot_tn(s1, qc[HALF:, cols])
        cg[1, :HALF, cols] = kk[:HALF] + dot_tn(s0, qc[:HALF, cols])
        cg[1, HALF:GROUP, cols] = kk[HALF:]
        vv = dot_tn(p1[h], o1)
        cg[2, :HALF, cols] = vv[:HALF] + dot_tn(p0[h], o0)
        cg[2, HALF:GROUP, cols] = vv[HALF:]
        return c

    over(0, mid, back)
    scan_slices(True, bs, b1_s, br, b1_r, bo, bi, b2_s, b2_r)
    over(mid, heads, back)

    def edge(c):
        return ctx_copy(
            cg.at[c, pl.ds(0, 8), :], cg.at[c, pl.ds(GROUP, 8), :],
            eh_s.at[c], eh_r.at[c], lax.rem(me + n - 1, n),
        )

    @pl.when(me == n - 1)
    def _():
        cg[:, pl.ds(GROUP, 8), :] = jnp.zeros((3, 8, width), F32)

    @pl.when(me > 0)
    def _():
        edge(0).start()

    def taps(c, h):
        cols = cols_of(h)
        part = cg[c, :GROUP, cols]
        for j in range(TAPS):
            r = c * TAPS + j
            tap[(r // 8) * heads + h, r % 8 : r % 8 + 1, :] = jnp.sum(
                part * xf[c, pl.ds(PAD - j, GROUP), cols], axis=0, keepdims=True
            )

    def q_taps(h, c):
        taps(0, h)
        return c

    over(0, heads, q_taps)

    @pl.when(me < n - 1)
    def _():
        edge(0).wait_recv()

    def unconv(c):
        def one(h, carry):
            cols = cols_of(h)
            y = w_ref[c, 0:1, cols] * cg[c, pl.ds(0, GROUP), cols]
            for j in range(1, TAPS):
                y = y + w_ref[c, j : j + 1, cols] * cg[c, pl.ds(j, GROUP), cols]
            outb[c, :, cols] = y.astype(BF16)
            return carry

        over(0, heads, one)

    outs = [
        pltpu.make_async_copy(outb.at[c], dst, loc.at[5 + c])
        for c, dst in enumerate((qg_hbm, kg_hbm, vg_hbm))
    ]
    unconv(0)
    outs[0].start()
    await_states(bo, bi, b2_s, b2_r)

    def late(h, c):
        cols = cols_of(h)
        state = state_of(bi, h)
        sh = shrink_of(h)
        cg[1, :GROUP, cols] += dot_nt(vc[:, cols], state) * sh
        cg[2, :GROUP, cols] += dot_nn(kc[:, cols], state) * sh
        return c

    over(0, heads, late)

    @pl.when(me > 0)
    def _():
        edge(1).start()
        edge(2).start()

    def kv_taps(h, c):
        taps(1, h)
        taps(2, h)
        return c

    over(0, heads, kv_taps)

    def tap_copy(o, source):
        return ctx_copy(tap.at[o], tapr.at[source], t1_s.at[o], t1_r.at[source], o)

    peers(tiles, lambda o: tap_copy(o, me).start())

    @pl.when(me < n - 1)
    def _():
        for c in (1, 2):
            edge(c).wait_recv()

    unconv(1)
    outs[1].start()

    def sum_copy(p, source):
        return ctx_copy(tsum, tapo.at[source], t2_s.at[p], t2_r.at[source], p)

    def own_sum():
        tapr[me] = tap[me]
        peers(n, lambda s: tap_copy(0, s).wait_recv())
        tsum[...] = lax.fori_loop(0, n, lambda s, a: a + tapr[s], jnp.zeros((8, HD), F32))
        tapo[me] = tsum[...]
        peers(n, lambda p: sum_copy(p, me).start())

    owning(tiles, own_sum)
    unconv(2)
    outs[2].start()
    peers(tiles, lambda o: sum_copy(0, o).wait_recv())
    for h in range(heads):
        cols = slice(h * HD, (h + 1) * HD)
        low, high = tapo[h], tapo[heads + h]
        cgrad_ref[0, :, cols] = low[0:4]
        cgrad_ref[1, :, cols] = low[4:8]
        cgrad_ref[2, :, cols] = high[0:4]
        ggrad_ref[0:1, cols] = high[4:5]

    @pl.when(me < n - 1)
    def _():
        for c in range(3):
            halo(c).wait_send()

    @pl.when(me > 0)
    def _():
        for c in range(3):
            edge(c).wait_send()

    def sent_to_owner(o):
        clos_copy(o, me).wait_send()
        slice_copy(fs, fr, f1_s, f1_r, o, me).wait_send()
        slice_copy(bs, br, b1_s, b1_r, o, me).wait_send()

    peers(owners, sent_to_owner)

    def sent_states():
        def one(p):
            ctx_copy(fo.at[p], fi.at[me], f2_s.at[p], f2_r.at[me], p).wait_send()
            ctx_copy(bo.at[p], bi.at[me], b2_s.at[p], b2_r.at[me], p).wait_send()

        peers(n, one)

    owning(owners, sent_states)
    for d in range(1, m):
        sums_copy(lax.rem(hme + d, m), hme).wait_send()
    peers(tiles, lambda o: tap_copy(o, me).wait_send())
    owning(tiles, lambda: peers(n, lambda p: sum_copy(p, me).wait_send()))
    mix_out.wait()
    for cp in outs:
        cp.wait()


PIECES = 4


def hand_on(*refs):
    count = (len(refs) - 3) // 2
    srcs, dsts = refs[:count], refs[count : 2 * count]
    stage, got, put = refs[-3:]
    step = GROUP // PIECES
    loads, stores = [], []
    for j in range(PIECES):
        part = pl.ds(j * step, step)
        for i in range(4):
            k = i * PIECES + j
            loads.append(
                pltpu.make_async_copy(srcs[i].at[part, :], stage.at[i, part, :], got.at[k])
            )
            stores.append(
                pltpu.make_async_copy(stage.at[i, part, :], dsts[i].at[part, :], put.at[k])
            )
    for cp in loads:
        cp.start()
    for i in range(4, count):
        dsts[i][...] = srcs[i][...]
    for cp, out in zip(loads, stores):
        cp.wait()
        out.start()
    for out in stores:
        out.wait()


def body(n, m, query_rows, key_rows, value_rows, log_gate, conv_weight, norm_gain, mixed_grad):
    tok_here, width = query_rows.shape
    assert tok_here == GROUP
    heads = width // HD
    owners = min(n, width // 16)
    per = owners // heads
    R = HD // per
    tiles = 2 * heads
    assert tiles <= n
    if heads < 8:
        log_gate = jnp.pad(log_gate, ((0, 8 - heads), (0, 0)))
    any_ = pl.BlockSpec(memory_space=pl.ANY)
    vm = pl.BlockSpec(memory_space=pltpu.VMEM)
    V = pltpu.VMEM
    S = pltpu.SemaphoreType.DMA
    rows = jax.ShapeDtypeStruct((GROUP, width), BF16)
    result = pl.pallas_call(
        functools.partial(kernel, n, m, heads, owners),
        out_shape=(
            rows, rows, rows, rows,
            jax.ShapeDtypeStruct((3, TAPS, width), F32),
            jax.ShapeDtypeStruct((1, width), F32),
        ),
        in_specs=[any_] * 4 + [vm] * 3,
        out_specs=(any_, any_, any_, any_, vm, vm),
        scratch_shapes=[
            V((3, PAD + GROUP, width), BF16),
            V((3, PAD + GROUP, width), F32),
            V((GROUP, width), BF16),
            V((GROUP, width), BF16),
            V((GROUP, width), BF16),
            V((GROUP, width), BF16),
            V((GROUP, width), F32),
            V((GROUP, width), BF16),
            V((GROUP, width), BF16),
            V((3, GROUP, width), BF16),
            V((3, GROUP + 8, width), F32),
            V((heads, HALF, HALF), F32),
            V((heads, HALF, GROUP), F32),
            V((heads, HALF, HALF), BF16),
            V((heads, HALF, GROUP), BF16),
            V((heads, GROUP, HD), F32),
            V((heads, 8, GROUP), F32),
            V((heads, 8, HD), F32),
            V((n, 8, HD), F32),
            V((owners, R, HD), BF16),
            V((n, R, HD), BF16),
            V((n, R, HD), BF16),
            V((owners, R, HD), BF16),
            V((owners, R, HD), BF16),
            V((n, R, HD), BF16),
            V((n, R, HD), BF16),
            V((owners, R, HD), BF16),
            V((GROUP, HD), F32),
            V((GROUP, HD), F32),
            V((GROUP, HD), F32),
            V((GROUP, HD), F32),
            V((8, GROUP), F32),
            V((m, 8, GROUP), F32),
            V((tiles, 8, HD), F32),
            V((n, 8, HD), F32),
            V((8, HD), F32),
            V((tiles, 8, HD), F32),
            S((8,)), S((3,)), S((3,)), S((n,)), S((n,)),
            S((n,)), S((n,)), S((n,)), S((n,)),
            S((n,)), S((n,)), S((n,)), S((n,)),
            S((m,)), S((m,)), S((3,)), S((3,)),
            S((n,)), S((n,)), S((n,)), S((n,)),
        ],
        compiler_params=pltpu.CompilerParams(
            collective_id=0, has_side_effects=True, vmem_limit_bytes=60 * 1024 * 1024
        ),
    )(
        query_rows, key_rows, value_rows, mixed_grad,
        log_gate, conv_weight, norm_gain.reshape(1, width),
    )
    specs = [any_] * 4 + [vm] * 2
    result = pl.pallas_call(
        hand_on,
        out_shape=tuple(jax.ShapeDtypeStruct(r.shape, r.dtype) for r in result),
        in_specs=specs,
        out_specs=tuple(specs),
        scratch_shapes=[V((4, GROUP, width), BF16), S((4 * PIECES,)), S((4 * PIECES,))],
    )(*result)
    return (*result[:5], result[5].reshape(width))


def solution(mesh):
    n, m = mesh.shape["ctx"], mesh.shape["head"]
    rows = P("ctx", "head")
    return jax.shard_map(
        functools.partial(body, n, m),
        mesh=mesh,
        in_specs=(rows, rows, rows, P("head", "ctx"), P(None, None, "head"), P("head"), rows),
        out_specs=(rows, rows, rows, rows, P(None, None, "head"), P("head")),
        check_vma=False,
    )
```
